32 devices in a mesh: occ: 4 (over y, x), vir: 8 (over z, core).
Axes of the slice: x: 2, y: 2, z: 4, core: 2. Of those that a mesh axis runs over, the one named last changes fastest.
Arguments:
- amplitudes: bfloat16 [2048, 16384], P('occ', 'vir'), may hold values from -6 to 6
- integrals: bfloat16 [16384, 512], P('vir', 'occ'), may hold values from -0.09375 to 0.09375
- active: int32 [16, 128], P('occ', 'vir'), may hold values from 0 to 1
Outputs:
- residual: bfloat16 [2048, 512], P('occ', 'vir')
The draws below stay inside these ranges and needn't reach their ends.
All inputs are finite; a program needn't handle non-finite values.
Results may differ from the reference program's by a relative error of at most 0.001.
Values may be sent and summed in bfloat16 or wider, within the bound.
A program may use at most 64 MiB of HBM per device.

```python
import jax
import jax.numpy as jnp
from jax import lax

TILE = 128
OCC_TILES = 16
EF_COUNT = 128
OCC_ROWS = 2048
EF_PAIRS = 16384
AB_PAIRS = 512


def draw_active(key, part):
    tile_index = jnp.arange(OCC_TILES, dtype=jnp.int32)[:, None]
    level = 1 + 6 * tile_index // max(OCC_TILES - 1, 1)
    draws = jax.random.randint(key, (OCC_TILES, EF_COUNT), 0, 8)
    return (draws < level).astype(jnp.int32)


def spiked(values, own_key, source, target, parts, factor):
    def block_of(dim):
        return (jnp.arange(values.shape[dim]) // (values.shape[dim] // parts)).reshape((-1,) + (1,) * (values.ndim - 1 - dim))

    one_side = jax.random.permutation(own_key, parts)[block_of(target)]
    other_side = (block_of(target) + parts // 2) % parts
    return jnp.where((block_of(source) == one_side) | (block_of(source) == other_side), factor * values, values)


def shard_levels(key, shape, pieces, smallest, top_value):
    def one(axis_at, shards_of):
        steps = jax.random.uniform(jax.random.fold_in(jax.random.fold_in(key, 6), axis_at), (shards_of,), jnp.float32, smallest / len(pieces), top_value / len(pieces))
        return jnp.repeat(jnp.exp(steps), shape[axis_at] // shards_of).reshape((-1,) + (1,) * (len(shape) - axis_at - 1))

    level = one(*pieces[0])
    for cut in pieces[1:]:
        level = level * one(*cut)
    return level


def gaussian(rng, shape, deviation, most, pieces=(), held_as=jnp.bfloat16):
    values = deviation * jax.random.normal(rng, shape, jnp.float32)
    if pieces:
        values = values * shard_levels(rng, shape, pieces, -0.22, 0.18)
    return jnp.clip(values, -most, most).astype(held_as)


def gaussian_with(stream_key, shape, width, reach, pieces, heavy, kind=jnp.bfloat16):
    array = width * jax.random.normal(stream_key, shape, jnp.float32)
    if pieces:
        array = array * shard_levels(stream_key, shape, pieces, -0.22, 0.18)
    return jnp.clip(spiked(array, jax.random.fold_in(stream_key, 3), *heavy), -reach, reach).astype(kind)


def setup_inputs(seed: int = 0) -> dict:
    splits = jax.random.split(jax.random.key(seed), 4)
    amplitudes = gaussian(splits[0], (OCC_ROWS, EF_PAIRS), 1.0, 6.0, ((0, 4), (1, 8)))
    integrals = gaussian_with(splits[1], (EF_PAIRS, AB_PAIRS), (EF_PAIRS // 2) ** -0.5, 0.09375, ((0, 8), (1, 4)), (0, 1, 8, 2.0))
    active = draw_active(jax.random.fold_in(splits[3], 71), 0)
    return dict(amplitudes=amplitudes, integrals=integrals, active=active)


def reference(amplitudes, integrals, active):
    row_tiles = active.shape[0]
    pair_tiles = active.shape[1]
    blocks = amplitudes.reshape(row_tiles, TILE, pair_tiles, TILE)
    weights = active.astype(amplitudes.dtype)[:, None, :, None]
    masked = (blocks * weights).reshape(row_tiles, TILE, pair_tiles * TILE)

    def one_tile(rows):
        return jnp.dot(rows, integrals, preferred_element_type=jnp.float32).astype(jnp.bfloat16)

    result = lax.map(one_tile, masked)
    return result.reshape(row_tiles * TILE, integrals.shape[1])
```

```python
import functools
import math

import jax
import jax.numpy as jnp
from jax import lax
from jax.experimental import pallas as pl
from jax.experimental.pallas import tpu as pltpu
from jax.sharding import PartitionSpec as P

TILE = 128
MESH = pl.DeviceIdType.MESH


def fast_side(count):
    side = math.isqrt(count)
    while count % side:
        side -= 1
    return side


def kernel(
    p, q, nz, active, a_hbm, b_hbm, out, a, b, give, got, zsend, zrecv, total,
    a_sem, b_sem, own_sem, fwd_sem, recv_sem, give_sem, got_sem, zsend_sem, zrecv_sem,
):
    o = lax.axis_index("occ")
    v = lax.axis_index("vir")
    core, z = lax.rem(v, 2), lax.div(v, 2)
    pi, qi = lax.div(o, q), lax.rem(o, q)
    rows, depth = a.shape
    half = depth // 2
    width = b.shape[2]
    halves = (pl.ds(0, half), pl.ds(half, half))
    sibling = (o, v + 1 - 2 * core)

    def occ_at(dp, dq):
        return lax.rem(pi + dp, p) * q + lax.rem(qi + dq, q)

    def slot(dp, dq):
        return (dp % p) * q + dq % q

    a_copy = pltpu.make_async_copy(a_hbm, a, a_sem)
    a_copy.start()
    b_copy = pltpu.make_async_copy(b_hbm, b.at[0], b_sem)
    b_copy.start()

    barrier = pltpu.get_barrier_semaphore()
    peers = [sibling]
    peers += [(occ_at(0, d), v) for d in range(1, q)]
    peers += [(occ_at(d, 0), v) for d in range(1, p)]
    peers += [(o, lax.rem(z + d, nz) * 2 + core) for d in range(1, nz)]
    for peer in peers:
        pl.semaphore_signal(barrier, inc=1, device_id=peer, device_id_type=MESH)
    pl.semaphore_wait(barrier, len(peers))

    sends = []

    def send_own(dp, dq, h):
        copy = pltpu.make_async_remote_copy(
            src_ref=b_hbm.at[halves[h]],
            dst_ref=b.at[slot(-dp, -dq), halves[h]],
            send_sem=own_sem.at[slot(dp, dq), h],
            recv_sem=recv_sem.at[slot(-dp, -dq), h],
            device_id=(occ_at(dp, dq), v),
            device_id_type=MESH,
        )
        copy.start()
        sends.append(copy)

    def forward(sp, sq, dp, dq, h):
        copy = pltpu.make_async_remote_copy(
            src_ref=b.at[slot(sp, sq), halves[h]],
            dst_ref=b.at[slot(sp - dp, sq - dq), halves[h]],
            send_sem=fwd_sem.at[slot(sp + dp, sq + dq), h],
            recv_sem=recv_sem.at[slot(sp - dp, sq - dq), h],
            device_id=(occ_at(dp, dq), v),
            device_id_type=MESH,
        )
        copy.start()
        sends.append(copy)

    def arrived(dp, dq, h):
        place = b.at[slot(dp, dq), halves[h]]
        pltpu.make_async_copy(place, place, recv_sem.at[slot(dp, dq), h]).wait()

    for d in range(1, q):
        send_own(0, d, 0)
    for d in range(1, p):
        send_own(d, 0, 1)
    for d in range(1, q):
        send_own(0, d, 1)
    for d in range(1, p):
        send_own(d, 0, 0)

    a_copy.wait()
    for r in range(rows // TILE):
        for e in range(depth // TILE):
            place = (pl.ds(r * TILE, TILE), pl.ds(e * TILE, TILE))
            weight = active[r, e].astype(jnp.float32)
            a[place] = (a[place].astype(jnp.float32) * weight).astype(a.dtype)

    low = lax.broadcasted_iota(jnp.int32, (rows // 2, width), 1) < width // 2

    def multiply(dp, dq):
        s = slot(dp, dq)
        part = jnp.dot(a[...], b[s], preferred_element_type=jnp.float32)
        top, bottom = part[: rows // 2], part[rows // 2 :]
        for_first = jnp.where(low, top, pltpu.roll(bottom, width // 2, 1))
        for_second = jnp.where(low, pltpu.roll(top, width // 2, 1), bottom)
        first = core == 0
        give[s] = jnp.where(first, for_second, for_first)
        zsend[s] = jnp.where(first, for_first, for_second)
        copy = pltpu.make_async_remote_copy(
            src_ref=give.at[s],
            dst_ref=got.at[s],
            send_sem=give_sem.at[s],
            recv_sem=got_sem.at[s],
            device_id=sibling,
            device_id_type=MESH,
        )
        copy.start()
        return copy

    def z_copy(dp, dq):
        s = slot(dp, dq)
        owner = occ_at(dp, dq)
        place = lax.rem(z - owner + nz, nz)
        return pltpu.make_async_remote_copy(
            src_ref=zsend.at[s],
            dst_ref=zrecv.at[place],
            send_sem=zsend_sem.at[s],
            recv_sem=zrecv_sem.at[place],
            device_id=(o, owner * 2 + core),
            device_id_type=MESH,
        )

    def hand_over(dp, dq, copy):
        s = slot(dp, dq)
        copy.wait()
        owner = occ_at(dp, dq)

        @pl.when(owner == z)
        def _():
            total[...] = zsend[s] + got[s]

        @pl.when(owner != z)
        def _():
            zsend[s] = zsend[s] + got[s]
            z_copy(dp, dq).start()

    b_copy.wait()
    hand_over(0, 0, multiply(0, 0))

    for d in range(1, q):
        arrived(0, d, 0)
        for f in range(1, p):
            forward(0, d, f, 0, 0)
    for d in range(1, p):
        arrived(d, 0, 1)
        for f in range(1, q):
            forward(d, 0, 0, f, 1)

    near = []
    for d in range(1, q):
        arrived(0, d, 1)
        near.append((0, d, multiply(0, d)))
    for d in range(1, p):
        arrived(d, 0, 0)
        near.append((d, 0, multiply(d, 0)))
    for item in near:
        hand_over(*item)
    for dp in range(1, p):
        for dq in range(1, q):
            arrived(dp, dq, 0)
            arrived(dp, dq, 1)
            hand_over(dp, dq, multiply(dp, dq))

    result = total[...]
    for d in range(1, nz):
        pltpu.make_async_copy(zrecv.at[d], zrecv.at[d], zrecv_sem.at[d]).wait()
        result = result + zrecv[d]
    out[: rows // 2] = result[:, : width // 2].astype(out.dtype)
    out[rows // 2 :] = pltpu.roll(result, width // 2, 1)[:, : width // 2].astype(out.dtype)

    for copy in sends:
        copy.wait_send()
    for dp in range(p):
        for dq in range(q):

            @pl.when(occ_at(dp, dq) != z)
            def _():
                z_copy(dp, dq).wait_send()


def on_device(nocc, nvir, amplitudes, integrals, active):
    rows, depth = amplitudes.shape
    width = integrals.shape[1]
    q = fast_side(nocc)
    p = nocc // q
    nz = nvir // 2
    piece = (rows // 2, width)
    f32 = jnp.float32
    any_space = pl.BlockSpec(memory_space=pl.ANY)
    dma = pltpu.SemaphoreType.DMA
    return pl.pallas_call(
        functools.partial(kernel, p, q, nz),
        out_shape=jax.ShapeDtypeStruct((rows, width // 2), jnp.bfloat16),
        in_specs=[pl.BlockSpec(memory_space=pltpu.SMEM), any_space, any_space],
        out_specs=pl.BlockSpec(memory_space=pltpu.VMEM),
        scratch_shapes=[
            pltpu.VMEM((rows, depth), amplitudes.dtype),
            pltpu.VMEM((nocc, depth, width), integrals.dtype),
            pltpu.VMEM((nocc,) + piece, f32),
            pltpu.VMEM((nocc,) + piece, f32),
            pltpu.VMEM((nocc,) + piece, f32),
            pltpu.VMEM((nz,) + piece, f32),
            pltpu.VMEM(piece, f32),
            dma(()), dma(()),
            dma((nocc, 2)), dma((nocc, 2)), dma((nocc, 2)),
            dma((nocc,)), dma((nocc,)), dma((nocc,)), dma((nz,)),
        ],
        compiler_params=pltpu.CompilerParams(collective_id=0, has_side_effects=True),
    )(active, amplitudes, integrals)


def solution(mesh):
    nocc, nvir = mesh.shape["occ"], mesh.shape["vir"]
    return jax.shard_map(
        functools.partial(on_device, nocc, nvir),
        mesh=mesh,
        in_specs=(P("occ", "vir"), P("vir", "occ"), P("occ", "vir")),
        out_specs=P("occ", "vir"),
        check_vma=False,
    )
```

```python
import functools
import math

import jax
import jax.numpy as jnp
from jax import lax
from jax.experimental import pallas as pl
from jax.experimental.pallas import tpu as pltpu
from jax.sharding import PartitionSpec as P

TILE = 128
CHUNKS = 4
MESH = pl.DeviceIdType.MESH


def fast_side(count):
    side = math.isqrt(count)
    while count % side:
        side -= 1
    return side


def kernel(
    p, q, nz, active, a_hbm, b_hbm, out, a, raw, b, part, got, zsend, zrecv,
    a_sem, b_sem, own_sem, fwd_sem, recv_sem, give_sem, got_sem, zsend_sem, zrecv_sem, reach_sem,
):
    o = lax.axis_index("occ")
    v = lax.axis_index("vir")
    core, z = lax.rem(v, 2), lax.div(v, 2)
    pi, qi = lax.div(o, q), lax.rem(o, q)
    rows, depth = a.shape
    width = raw.shape[1]
    sub = width // CHUNKS
    deep = depth // CHUNKS
    tall = rows // CHUNKS
    short = tall // 2
    per_core = CHUNKS // 2
    halves = (pl.ds(0, deep // 2), pl.ds(deep // 2, deep // 2))
    sibling = (o, v + 1 - 2 * core)
    below, above = (o, v - 2), (o, v + 2)
    f32 = jnp.float32

    def occ_at(dp, dq):
        return lax.rem(pi + dp, p) * q + lax.rem(qi + dq, q)

    def slot(dp, dq):
        return (dp % p) * q + dq % q

    def signal(sem, peer):
        pl.semaphore_signal(sem, inc=1, device_id=peer, device_id_type=MESH)

    b_copy = pltpu.make_async_copy(b_hbm, raw, b_sem)
    b_copy.start()
    a_copy = pltpu.make_async_copy(a_hbm, a, a_sem)
    a_copy.start()

    barrier = pltpu.get_barrier_semaphore()
    near = [sibling]
    near += [(occ_at(0, d), v) for d in range(1, q)]
    near += [(occ_at(d, 0), v) for d in range(1, p)]
    for peer in near:
        signal(barrier, peer)
    pl.when(z > 0)(lambda: signal(barrier, below))
    pl.when(z < nz - 1)(lambda: signal(barrier, above))

    def group_of(shape):
        return lax.div(lax.broadcasted_iota(jnp.int32, shape, 1), sub)

    b_copy.wait()
    group = group_of((deep, width))
    quarters = [raw[k * deep : (k + 1) * deep].astype(f32) for k in range(CHUNKS)]
    for j in range(CHUNKS):
        packed = None
        for k in range(CHUNKS):
            turn = (sub * (k - j)) % width
            piece = pltpu.roll(quarters[k], turn, 1) if turn else quarters[k]
            packed = piece if packed is None else jnp.where(group == k, piece, packed)
        b[0, j] = packed.astype(b.dtype)

    beside = lax.div(z + nz - 1, nz) + lax.div(2 * nz - 2 - z, nz)
    pl.semaphore_wait(barrier, len(near) + beside)

    sends = []

    def remote(src, dst, send_sem, to_sem, peer):
        copy = pltpu.make_async_remote_copy(
            src_ref=src, dst_ref=dst, send_sem=send_sem, recv_sem=to_sem,
            device_id=peer, device_id_type=MESH,
        )
        copy.start()
        return copy

    def send_own(j, stage):
        if j >= CHUNKS:
            return
        moves = [(0, d, stage) for d in range(1, q)] + [(d, 0, 1 - stage) for d in range(1, p)]
        for dp, dq, h in moves:
            s = slot(-dp, -dq)
            sends.append(
                remote(
                    b.at[0, j, halves[h]], b.at[s, j, halves[h]],
                    own_sem.at[s, j, h], recv_sem.at[s, j, h], (occ_at(dp, dq), v),
                )
            )

    def forward(sp, sq, dp, dq, j, h):
        s, t = slot(sp, sq), slot(sp - dp, sq - dq)
        sends.append(
            remote(
                b.at[s, j, halves[h]], b.at[t, j, halves[h]],
                fwd_sem.at[t, j, h], recv_sem.at[t, j, h], (occ_at(dp, dq), v),
            )
        )

    def arrived(dp, dq, j, h):
        s = slot(dp, dq)
        place = b.at[s, j, halves[h]]
        pltpu.make_async_copy(place, place, recv_sem.at[s, j, h]).wait()

    def reach(step):
        pl.when(z > 0)(lambda: signal(reach_sem.at[step, 1], below))
        pl.when(z < nz - 1)(lambda: signal(reach_sem.at[step, 0], above))

    def reached(step):
        pl.when(z > 0)(lambda: pl.semaphore_wait(reach_sem.at[step, 0], 1))
        pl.when(z < nz - 1)(lambda: pl.semaphore_wait(reach_sem.at[step, 1], 1))

    send_own(0, 0)
    send_own(0, 1)
    send_own(1, 0)
    reach(0)

    a_copy.wait()
    for r in range(rows // TILE):
        for e in range(depth // TILE):
            place = (pl.ds(r * TILE, TILE), pl.ds(e * TILE, TILE))
            weight = active[r, e].astype(f32)
            a[place] = (a[place].astype(f32) * weight).astype(a.dtype)

    for step in range(1, nz - 1):
        reached(step - 1)
        reach(step)
    lanes = group_of((tall, width))

    def multiply(dp, dq, j):
        s = slot(dp, dq)
        block = b[s, j]
        parts = [
            jnp.dot(a[:, k * deep : (k + 1) * deep], block, preferred_element_type=f32)
            for k in range(CHUNKS)
        ]
        summed = None
        for d in range(CHUNKS):
            mixed = None
            for k in range(CHUNKS):
                r = (k + d) % CHUNKS
                piece = parts[k][r * tall : (r + 1) * tall]
                mixed = piece if mixed is None else jnp.where(lanes == k, piece, mixed)
            mixed = pltpu.roll(mixed, sub * d, 1) if d else mixed
            summed = mixed if summed is None else summed + mixed
        part[s, j, 0] = summed[:short]
        part[s, j, 1] = summed[short:]
        copy = remote(
            part.at[s, j, 1 - core], got.at[s, j], give_sem.at[s, j], got_sem.at[s, j], sibling
        )
        return dp, dq, j, copy

    def z_copy(dp, dq, j):
        s = slot(dp, dq)
        owner = occ_at(dp, dq)
        place = lax.rem(z - owner + nz, nz)
        keeper = j // per_core
        return pltpu.make_async_remote_copy(
            src_ref=zsend.at[s, j],
            dst_ref=zrecv.at[j % per_core, place, core],
            send_sem=zsend_sem.at[s, j],
            recv_sem=zrecv_sem.at[j % per_core, place, core],
            device_id=(o, owner * 2 + keeper),
            device_id_type=MESH,
        )

    def stays(dp, dq, j):
        return occ_at(dp, dq) * 2 + j // per_core == v

    def hand_over(dp, dq, j, copy):
        s = slot(dp, dq)
        copy.wait()
        value = part[s, j, core] + got[s, j]

        @pl.when(stays(dp, dq, j))
        def _():
            zrecv[j % per_core, 0, core] = value

        @pl.when(jnp.logical_not(stays(dp, dq, j)))
        def _():
            zsend[s, j] = value
            z_copy(dp, dq, j).start()

    pending = []

    def run(dp, dq, j):
        pending.append(multiply(dp, dq, j))
        while len(pending) > 1:
            hand_over(*pending.pop(0))

    def diagonals(j):
        for dp in range(1, p):
            for dq in range(1, q):
                arrived(dp, dq, j, 0)
                arrived(dp, dq, j, 1)
                run(dp, dq, j)

    first = multiply(0, 0, 0)
    pending.append(first)
    reached(nz - 2)
    for j in range(CHUNKS):
        for d in range(1, q):
            arrived(0, d, j, 0)
            for f in range(1, p):
                forward(0, d, f, 0, j, 0)
        for d in range(1, p):
            arrived(d, 0, j, 1)
            for f in range(1, q):
                forward(d, 0, 0, f, j, 1)
        send_own(j + 1, 1)
        send_own(j + 2, 0)
        if j:
            diagonals(j - 1)
        if j + 1 < CHUNKS:
            run(0, 0, j + 1)
        for d in range(1, q):
            arrived(0, d, j, 1)
            run(0, d, j)
        for d in range(1, p):
            arrived(d, 0, j, 0)
            run(d, 0, j)
    while pending:
        hand_over(*pending.pop(0))
    diagonals(CHUNKS - 1)
    while pending:
        hand_over(*pending.pop(0))

    sums = {}
    for g in range(per_core):
        for k in range(2):
            for d in range(nz):

                def wait(g=g, d=d, k=k):
                    place = zrecv.at[g, d, k]
                    pltpu.make_async_copy(place, place, zrecv_sem.at[g, d, k]).wait()

                if d:
                    wait()
                else:
                    pl.when(core != k)(wait)
            total = zrecv[g, 0, k]
            for d in range(1, nz):
                total = total + zrecv[g, d, k]
            sums[g, k] = total
    small = group_of((short, width))
    for r in range(CHUNKS):
        for k in range(2):
            value = None
            for g in range(per_core):
                turn = (sub * (g - r)) % width
                piece = pltpu.roll(sums[g, k], turn, 1) if turn else sums[g, k]
                value = piece if value is None else jnp.where(small == g, piece, value)
            start = r * tall + k * short
            out[start : start + short] = value[:, : width // 2].astype(out.dtype)

    for copy in sends:
        copy.wait_send()
    for j in range(CHUNKS):
        for dp in range(p):
            for dq in range(q):

                @pl.when(jnp.logical_not(stays(dp, dq, j)))
                def _():
                    z_copy(dp, dq, j).wait_send()


def on_device(nocc, nvir, amplitudes, integrals, active):
    rows, depth = amplitudes.shape
    width = integrals.shape[1]
    q = fast_side(nocc)
    p = nocc // q
    nz = nvir // 2
    g = CHUNKS
    short = rows // g // 2
    f32 = jnp.float32
    any_space = pl.BlockSpec(memory_space=pl.ANY)
    dma = pltpu.SemaphoreType.DMA
    return pl.pallas_call(
        functools.partial(kernel, p, q, nz),
        out_shape=jax.ShapeDtypeStruct((rows, width // 2), jnp.bfloat16),
        in_specs=[pl.BlockSpec(memory_space=pltpu.SMEM), any_space, any_space],
        out_specs=pl.BlockSpec(memory_space=pltpu.VMEM),
        scratch_shapes=[
            pltpu.VMEM((rows, depth), amplitudes.dtype),
            pltpu.VMEM((depth, width), integrals.dtype),
            pltpu.VMEM((nocc, g, depth // g, width), integrals.dtype),
            pltpu.VMEM((nocc, g, 2, short, width), f32),
            pltpu.VMEM((nocc, g, short, width), f32),
            pltpu.VMEM((nocc, g, short, width), f32),
            pltpu.VMEM((g // 2, nz, 2, short, width), f32),
            dma(()), dma(()),
            dma((nocc, g, 2)), dma((nocc, g, 2)), dma((nocc, g, 2)),
            dma((nocc, g)), dma((nocc, g)), dma((nocc, g)), dma((g // 2, nz, 2)),
            pltpu.SemaphoreType.REGULAR((nz - 1, 2)),
        ],
        compiler_params=pltpu.CompilerParams(collective_id=0, has_side_effects=True),
    )(active, amplitudes, integrals)


def solution(mesh):
    nocc, nvir = mesh.shape["occ"], mesh.shape["vir"]
    return jax.shard_map(
        functools.partial(on_device, nocc, nvir),
        mesh=mesh,
        in_specs=(P("occ", "vir"), P("vir", "occ"), P("occ", "vir")),
        out_specs=P("occ", "vir"),
        check_vma=False,
    )
```
